32 devices in a mesh: req: 8 (over z, x), mp: 4 (over y, core).
Axes of the slice: x: 2, y: 2, z: 4, core: 2. Of those that a mesh axis runs over, the one named last changes fastest.
Arguments:
- hidden: bfloat16 [2048, 4096], P(('req', 'mp')), may hold values from -4 to 4
- queries: bfloat16 [2048, 2048], P('req', 'mp'), may hold values from -130 to 130
- rotated_rollout_keys: bfloat16 [2048, 2, 128], P('req'), may hold values from -4 to 4
- rollout_value_matrix: bfloat16 [2048, 2, 128], P('req'), may hold values from -4 to 4
- cached_key_slabs: bfloat16 [16384, 2, 128], P('req'), may hold values from -4 to 4
- cached_value_slabs: bfloat16 [16384, 2, 128], P('req'), may hold values from -4 to 4
- out_weight: bfloat16 [2048, 4096], P('mp'), may hold values from -0.5 to 0.5
- final_gain: float32 [4096], replicated, may hold values from 0.1 to 1.9
- head_weight: bfloat16 [4096, 32000], P(None, 'req'), may hold values from -1 to 1
- token_ids: int32 [2048], P(('req', 'mp')), may hold values from 0 to 31999
- rollout_len: int32 [8], P('req'), may hold values from 64 to 256
- piece_offset: int32 [8], P('req'), may hold values from 0 to 3
- piece_len: int32 [8], P('req'), may hold values from 256 to 2048
Outputs:
- logprob: float32 [2048], P(('req', 'mp'))
- entropy: float32 [2048], P(('req', 'mp'))
The draws below stay inside these ranges and needn't reach their ends.
All inputs are finite; a program needn't handle non-finite values.
Results may differ from the reference program's by a relative error of at most 0.0045.
Values may be sent and summed in bfloat16 or wider, within the bound.
No kernel may reach another device: no remote copies, remote signals or barrier semaphores. Data moves between devices by JAX's collectives and lax.ppermute only.
A program may use at most 128 MiB of HBM per device.

```python
import math
import jax
import jax.numpy as jnp
import numpy as np
from jax import lax

D = 4096
HEAD_DIMENSION = 128
QUERY_HEADS = 16
KEY_VALUE_HEADS = 2
V = 32000
REQUEST_ROWS = 256
SLAB_POSITIONS = 2048
REACH = 4
REQUEST_GROUPS = 8
ROLLOUT_ROWS = 2048
CACHE_POSITIONS = 16384


def attention_pair(key):
    leading_slab, second = jax.random.split(jax.random.fold_in(key, 7))
    appended_keys = jax.random.truncated_normal(leading_slab, -4.0, 4.0, (ROLLOUT_ROWS, KEY_VALUE_HEADS, HEAD_DIMENSION), jnp.float32)
    query = jax.random.truncated_normal(second, -4.0, 4.0, (ROLLOUT_ROWS, QUERY_HEADS, HEAD_DIMENSION), jnp.float32)
    return (query.reshape(ROLLOUT_ROWS, QUERY_HEADS * HEAD_DIMENSION), appended_keys)


def vocabulary_pair(key):
    leading_slab, second = jax.random.split(jax.random.fold_in(key, 11))
    rows = jax.random.truncated_normal(leading_slab, -4.0, 4.0, (ROLLOUT_ROWS, D), jnp.float32)
    weights = jax.random.truncated_normal(second, -4.0, 4.0, (D, V), jnp.float32) * (3.0 / D ** 0.5)
    return (rows, weights)


def draw_queries(key, part):
    return attention_pair(key)[0].astype(jnp.bfloat16)


def draw_rotated_rollout_keys(key, part):
    return attention_pair(key)[1].astype(jnp.bfloat16)


def draw_hidden(key, part):
    return vocabulary_pair(key)[0].astype(jnp.bfloat16)


def draw_head_weight(key, part):
    return vocabulary_pair(key)[1].astype(jnp.bfloat16)


def touch_ends(values, stream_key, least, top_value):
    longest = values.shape.index(max(values.shape))
    spots = []
    for shift in (0, 1):
        where = [jax.random.randint(jax.random.fold_in(stream_key, axis), (), 0, length) for axis, length in enumerate(values.shape)]
        where[longest] = (where[longest] + shift) % values.shape[longest]
        spots.append(tuple(where))
    return values.at[spots[0]].set(least).at[spots[1]].set(top_value)


def steps_of(key, dims, shards, least, top_value):
    level, own = 1.0, jax.random.fold_in(key, 6)
    for position, blocks in shards:
        heights = jnp.exp(jax.random.uniform(jax.random.fold_in(own, position), (blocks,), jnp.float32, least / len(shards), top_value / len(shards)))
        level = level * jnp.repeat(heights, dims[position] // blocks).reshape([-1 if axis == position else 1 for axis in range(len(dims))])
    return level


def rank_table(amount, lean):
    portions = [(1 << 20) // math.isqrt(standing ** lean) + 1 for standing in range(1, amount + 1)]
    deviation = 1 + sum(portions) // (1 << 30)
    return np.cumsum(np.array([max(1, weight // deviation) for weight in portions]))


def skewed_ids(stream_key, extent, number_of, slope):
    grid = rank_table(number_of, slope)
    lot = jax.random.randint(jax.random.fold_in(stream_key, 1), extent, 0, int(grid[number_of - 1]))
    rank = jnp.searchsorted(jnp.asarray(grid, jnp.int32), lot, side="right")
    return jax.random.permutation(jax.random.fold_in(stream_key, 2), number_of)[rank].astype(jnp.int32)


def centred(stream_key, shape, deviation, most, cuts=(), kind=jnp.bfloat16):
    gain = steps_of(stream_key, shape, cuts, -0.22, 0.18) if cuts else 1.0
    values = jax.random.normal(stream_key, shape, jnp.float32) * deviation * gain
    return jnp.minimum(jnp.maximum(values, -most), most).astype(kind)


def setup_inputs(seed: int = 0) -> dict:
    arg_keys = jax.random.split(jax.random.key(seed), 14)
    hidden = draw_hidden(jax.random.fold_in(arg_keys[13], 71), 0)
    queries = draw_queries(jax.random.fold_in(arg_keys[13], 71), 0)
    rotated_rollout_keys = draw_rotated_rollout_keys(jax.random.fold_in(arg_keys[13], 71), 0)
    rollout_value_matrix = centred(arg_keys[3], (ROLLOUT_ROWS, KEY_VALUE_HEADS, HEAD_DIMENSION), 1.0, 4.0, ((0, 8),))
    cached_key_slabs = centred(arg_keys[4], (CACHE_POSITIONS, KEY_VALUE_HEADS, HEAD_DIMENSION), 1.0, 4.0, ((0, 8),))
    cached_value_slabs = centred(arg_keys[5], (CACHE_POSITIONS, KEY_VALUE_HEADS, HEAD_DIMENSION), 1.0, 4.0, ((0, 8),))
    out_weight = centred(arg_keys[6], (QUERY_HEADS * HEAD_DIMENSION, D), HEAD_DIMENSION ** -0.5, 0.5, ((0, 4),))
    final_gain = jnp.clip(1.0 + 0.18 * jax.random.normal(arg_keys[7], (D,), jnp.float32), 0.1, 1.9)
    head_weight = draw_head_weight(jax.random.fold_in(arg_keys[13], 71), 0)
    token_ids = touch_ends(skewed_ids(arg_keys[9], (ROLLOUT_ROWS,), V, 2), jax.random.fold_in(arg_keys[9], 3), 0, V - 1).astype(jnp.int32)
    rollout_len = touch_ends(jax.random.randint(arg_keys[10], (REQUEST_GROUPS,), REQUEST_ROWS // 4, REQUEST_ROWS + 1), jax.random.fold_in(arg_keys[10], 1), REQUEST_ROWS // 4, REQUEST_ROWS).astype(jnp.int32)
    piece_offset = touch_ends(jax.random.randint(arg_keys[11], (REQUEST_GROUPS,), 0, REACH), jax.random.fold_in(arg_keys[11], 1), 0, REACH - 1).astype(jnp.int32)
    piece_len = touch_ends(jax.random.randint(arg_keys[12], (REQUEST_GROUPS,), SLAB_POSITIONS // 8, SLAB_POSITIONS + 1), jax.random.fold_in(arg_keys[12], 1), SLAB_POSITIONS // 8, SLAB_POSITIONS).astype(jnp.int32)
    return dict(hidden=hidden, queries=queries, rotated_rollout_keys=rotated_rollout_keys, rollout_value_matrix=rollout_value_matrix, cached_key_slabs=cached_key_slabs, cached_value_slabs=cached_value_slabs, out_weight=out_weight, final_gain=final_gain, head_weight=head_weight, token_ids=token_ids, rollout_len=rollout_len, piece_offset=piece_offset, piece_len=piece_len)


NEGATIVE = -1e+30

def softmax_part(query, keys, values, mask, factor):
    scores = jnp.einsum('thd,chd->thc', query, keys) * factor
    scores = jnp.where(mask[:, None, :], scores, NEGATIVE)
    top = lax.optimization_barrier(jnp.max(scores, axis=-1))
    weights = jnp.exp(scores - top[..., None])
    total = lax.optimization_barrier(jnp.sum(weights, axis=-1))
    rounded = weights.astype(jnp.bfloat16).astype(jnp.float32)
    summed = jnp.einsum('thc,chd->thd', rounded, values)
    return (top, total, summed)

def reference(hidden, queries, rotated_rollout_keys, rollout_value_matrix, cached_key_slabs, cached_value_slabs, out_weight, final_gain, head_weight, token_ids, rollout_len, piece_offset, piece_len):
    factor = 1.0 / math.sqrt(HEAD_DIMENSION)
    paired_heads = jnp.arange(QUERY_HEADS, dtype=jnp.int32) // (QUERY_HEADS // KEY_VALUE_HEADS)
    owners = (jnp.arange(REQUEST_GROUPS, dtype=jnp.int32) - piece_offset) % REQUEST_GROUPS
    query_all = queries.astype(jnp.float32).reshape(REQUEST_GROUPS, REQUEST_ROWS, QUERY_HEADS, HEAD_DIMENSION)
    current_slab_keys = cached_key_slabs.astype(jnp.float32).reshape(REQUEST_GROUPS, SLAB_POSITIONS, KEY_VALUE_HEADS, HEAD_DIMENSION)
    current_slab_values = cached_value_slabs.astype(jnp.float32).reshape(REQUEST_GROUPS, SLAB_POSITIONS, KEY_VALUE_HEADS, HEAD_DIMENSION)
    rollout_key_rows = rotated_rollout_keys.astype(jnp.float32).reshape(REQUEST_GROUPS, REQUEST_ROWS, KEY_VALUE_HEADS, HEAD_DIMENSION)
    rollout_value_rows = rollout_value_matrix.astype(jnp.float32).reshape(REQUEST_GROUPS, REQUEST_ROWS, KEY_VALUE_HEADS, HEAD_DIMENSION)
    positions = jnp.arange(SLAB_POSITIONS, dtype=jnp.int32)
    rows = jnp.arange(REQUEST_ROWS, dtype=jnp.int32)
    causal = rows[None, :] <= rows[:, None]

    def slab(index):
        query = query_all[owners[index]]
        keys = jnp.take(current_slab_keys[index], paired_heads, axis=1)
        values = jnp.take(current_slab_values[index], paired_heads, axis=1)
        mask = jnp.broadcast_to(positions < piece_len[index], (REQUEST_ROWS, SLAB_POSITIONS))
        return softmax_part(query, keys, values, mask, factor)
    slab_max, slab_total, slab_sum = lax.map(slab, jnp.arange(REQUEST_GROUPS, dtype=jnp.int32))

    def request(owner_index):
        keys = jnp.take(rollout_key_rows[owner_index], paired_heads, axis=1)
        values = jnp.take(rollout_value_rows[owner_index], paired_heads, axis=1)
        own_max, own_total, own_sum = softmax_part(query_all[owner_index], keys, values, causal, factor)
        hit = owners == owner_index
        far_top = jnp.where(hit[:, None, None], slab_max, NEGATIVE)
        top = jnp.maximum(own_max, lax.optimization_barrier(jnp.max(far_top, axis=0)))
        own_scale = jnp.exp(own_max - top)
        far_scale = jnp.exp(far_top - top)
        total = own_total * own_scale + lax.optimization_barrier(jnp.sum(slab_total * far_scale, axis=0))
        summed = own_sum * own_scale[..., None] + jnp.einsum('gth,gthd->thd', far_scale, slab_sum)
        mixed = (summed / total[..., None]).astype(jnp.bfloat16).reshape(REQUEST_ROWS, QUERY_HEADS * HEAD_DIMENSION)
        start = owner_index * REQUEST_ROWS
        rows_in = lax.dynamic_slice_in_dim(hidden, start, REQUEST_ROWS, 0)
        stream = rows_in.astype(jnp.float32) + jnp.dot(mixed, out_weight, preferred_element_type=jnp.float32)
        normed = (stream * lax.rsqrt(lax.optimization_barrier(jnp.mean(stream * stream, axis=-1, keepdims=True)) + 1e-06) * final_gain).astype(jnp.bfloat16)
        logits = jnp.dot(normed, head_weight, preferred_element_type=jnp.float32)
        peak = lax.optimization_barrier(jnp.max(logits, axis=-1, keepdims=True))
        spread = jnp.exp(logits - peak)
        whole = lax.optimization_barrier(jnp.sum(spread, axis=-1))
        log_total = peak[:, 0] + jnp.log(whole)
        mean_logit = lax.optimization_barrier(jnp.sum(spread * logits, axis=-1)) / whole
        words = lax.dynamic_slice_in_dim(token_ids, start, REQUEST_ROWS, 0)
        picked = jnp.take_along_axis(logits, words[:, None], axis=1)[:, 0]
        valid = rows < rollout_len[owner_index]
        return (jnp.where(valid, picked - log_total, 0.0), jnp.where(valid, log_total - mean_logit, 0.0))
    logprob, entropy = lax.map(request, jnp.arange(REQUEST_GROUPS, dtype=jnp.int32))
    return (logprob.reshape(ROLLOUT_ROWS), entropy.reshape(ROLLOUT_ROWS))
```

```python
import functools
import math

import jax
import jax.numpy as jnp
from jax import lax
from jax.experimental import pallas as pl
from jax.experimental.pallas import tpu as pltpu
from jax.sharding import PartitionSpec as P

NEGATIVE = -1e30
BLOCK = 256
META = 16
STATE = 8
MIB = 1 << 20


def ring_order(groups):
    wide = 1 << (int(math.log2(groups)) // 2)
    tall = groups // wide
    order = [z * wide for z in range(tall)]
    for step, z in enumerate(reversed(range(tall))):
        across = range(1, wide) if step % 2 == 0 else reversed(range(1, wide))
        order += [z * wide + x for x in across]
    return order


def nt(a, b):
    return lax.dot_general(a, b, (((1,), (1,)), ((), ())), preferred_element_type=jnp.float32)


def tn(a, b):
    return lax.dot_general(a, b, (((0,), (0,)), ((), ())), preferred_element_type=jnp.float32)


def put_state(state, head, size, top, total):
    rows = lax.broadcasted_iota(jnp.int32, (STATE, top.shape[1]), 0)
    state[head, size : size + STATE, :] = jnp.where(rows == 0, top, total)


def attend_slab(core, want, kv, query, state, size, scale):
    half = (kv.shape[0] - META) // 2
    heads = query.shape[1] // size
    meta = kv[2 * half : 2 * half + META, :].astype(jnp.float32)
    offset = jnp.max(meta[0:1, :]).astype(jnp.int32)
    length = jnp.max(meta[1:2, :] * 256.0 + meta[2:3, :]).astype(jnp.int32)
    blocks = jnp.clip((length - core * BLOCK + 2 * BLOCK - 1) // (2 * BLOCK), 0, half // BLOCK)
    blocks = jnp.where(offset == want, blocks, 0)

    def step(j, carry):
        start = pl.multiple_of(j * BLOCK, BLOCK)
        keys = kv[pl.ds(start, BLOCK), :]
        values = kv[pl.ds(half + start, BLOCK), :]
        place = lax.broadcasted_iota(jnp.int32, (BLOCK, 1), 0) + (2 * j + core) * BLOCK
        valid = place < length
        for h in range(heads):
            scores = nt(keys, query[:, h * size : (h + 1) * size]) * scale
            scores = jnp.where(valid, scores, NEGATIVE)
            before = state[h, size : size + 1, :]
            top = jnp.maximum(before, jnp.max(scores, axis=0, keepdims=True))
            old = jnp.exp2(before - top)
            weights = jnp.exp2(scores - top)
            total = state[h, size + 1 : size + 2, :] * old + jnp.sum(weights, axis=0, keepdims=True)
            state[h, :size, :] = state[h, :size, :] * old + tn(values, weights.astype(jnp.bfloat16))
            put_state(state, h, size, top, total)
        return carry

    lax.fori_loop(0, blocks, step, 0)


def first_kernel(sc, times, query, keys, values, kv, state, *, size, scale):
    core = sc[0]
    here = keys.shape[0]
    place = lax.broadcasted_iota(jnp.int32, (here, 1), 0) + core * here
    valid = place <= times[...]
    for h in range(query.shape[1] // size):
        scores = nt(keys[...], query[:, h * size : (h + 1) * size]) * scale
        scores = jnp.where(valid, scores, NEGATIVE)
        top = jnp.max(scores, axis=0, keepdims=True)
        weights = jnp.exp2(scores - top)
        state[h, :size, :] = tn(values[...], weights.astype(jnp.bfloat16))
        put_state(state, h, size, top, jnp.sum(weights, axis=0, keepdims=True))
    attend_slab(core, sc[1], kv, query, state, size, scale)


def more_kernel(sc, query, *refs, size, scale, slots, split):
    kvs, given, outs = refs[:slots], refs[slots], refs[slots + 1 :]
    if split:
        state = outs[2]
    else:
        state = outs[0]
    state[...] = given[...]
    for i, kv in enumerate(kvs):
        attend_slab(sc[0], sc[1 + i], kv, query, state, size, scale)
    if split:
        middle = state.shape[2] // 2
        outs[0][...] = state[:, :, :middle]
        outs[1][...] = state[:, :, middle:]


def merge_kernel(kept, came, mine, mate, own, send, mixed, *, size, rows):
    heads = kept.shape[0]

    @pl.when(pl.program_id(0) == 0)
    def _():
        for h in range(heads):
            other = (h + heads // 2) % heads
            first, second = kept[h, size : size + 1, :], came[other, size : size + 1, :]
            top = jnp.maximum(first, second)
            left, right = jnp.exp2(first - top), jnp.exp2(second - top)
            total = kept[h, size + 1 : size + 2, :] * left + came[other, size + 1 : size + 2, :] * right
            value = (kept[h, :size, :] * left + came[other, :size, :] * right) / total
            mixed[:, h * size : (h + 1) * size] = value.T.astype(jnp.bfloat16)

    width = mine.shape[0]
    out = jnp.dot(mixed[:, :width], mine[...], preferred_element_type=jnp.float32)
    out += jnp.dot(mixed[:, width:], mate[...], preferred_element_type=jnp.float32)
    own[...] = out[:rows, :]
    send[...] = out[rows:, :].astype(jnp.bfloat16)


def norm_kernel(own, hidden, gain, words, *refs):
    came, out = refs[:-1], refs[-1]
    stream = own[...] + hidden[...].astype(jnp.float32)
    for part in came:
        stream += part[...].astype(jnp.float32)
    width = stream.shape[1]
    square = jnp.sum(stream * stream, axis=1, keepdims=True) * (1.0 / width)
    out[:, :width] = (stream * lax.rsqrt(square + 1e-06) * gain[...]).astype(jnp.bfloat16)
    lane = lax.broadcasted_iota(jnp.int32, (stream.shape[0], out.shape[1] - width), 1)
    code = jnp.where(lane == 0, words[...] >> 8, words[...] & 255)
    out[:, width:] = code.astype(jnp.float32).astype(jnp.bfloat16)


def logits_kernel(sc, *refs, block):
    parts, weight, out, rows, codes = refs[:-4], refs[-4], refs[-3], refs[-2], refs[-1]
    width = weight.shape[1]
    at = 0
    for part in parts:
        rows[at : at + part.shape[0], :] = part[:, :width]
        codes[at : at + part.shape[0], :] = part[:, width:].astype(jnp.float32)
        at += part.shape[0]
    turned = codes[...].T
    words = (turned[0:1, :] * 256.0 + turned[1:2, :]).astype(jnp.int32) - sc[0]
    count = at
    place = lax.broadcasted_iota(jnp.int32, (block, 1), 0)

    def step(i, carry):
        top, total, weighted, picked = carry
        start = pl.multiple_of(i * block, 8)
        logits = nt(weight[pl.ds(start, block), :], rows[...])
        now = jnp.maximum(top, jnp.max(logits, axis=0, keepdims=True))
        old = jnp.exp(top - now)
        spread = jnp.exp(logits - now)
        total = total * old + jnp.sum(spread, axis=0, keepdims=True)
        weighted = weighted * old + jnp.sum(spread * logits, axis=0, keepdims=True)
        hit = place == words - start
        picked = picked + jnp.sum(jnp.where(hit, logits, 0.0), axis=0, keepdims=True)
        return now, total, weighted, picked

    zero = jnp.zeros((1, count), jnp.float32)
    carry = (jnp.full((1, count), NEGATIVE, jnp.float32), zero, zero, zero)
    top, total, weighted, picked = lax.fori_loop(0, weight.shape[0] // block, step, carry)
    line = lax.broadcasted_iota(jnp.int32, (STATE, count), 0)
    result = jnp.where(line == 0, top, jnp.where(line == 1, total, weighted))
    out[...] = jnp.where(line == 3, picked, result)


def smem():
    return pl.BlockSpec(memory_space=pltpu.SMEM)


def vmem():
    return pl.BlockSpec(memory_space=pltpu.VMEM)


def call(kernel, shapes, specs, limit, flops=0, read=0, **extra):
    return pl.pallas_call(
        kernel,
        out_shape=shapes,
        in_specs=specs,
        compiler_params=pltpu.CompilerParams(vmem_limit_bytes=limit * MIB),
        cost_estimate=pl.CostEstimate(flops=flops, bytes_accessed=read, transcendentals=0),
        **extra,
    )


def shape(dims, kind=jnp.float32):
    return jax.ShapeDtypeStruct(dims, kind)


def body(
    hidden,
    queries,
    rotated_rollout_keys,
    rollout_value_matrix,
    cached_key_slabs,
    cached_value_slabs,
    out_weight,
    final_gain,
    head_weight,
    token_ids,
    rollout_len,
    piece_offset,
    piece_len,
):
    groups, members = lax.axis_size("req"), lax.axis_size("mp")
    request, member = lax.axis_index("req"), lax.axis_index("mp")
    core = member % 2
    rollout, rows_here = queries.shape[0], hidden.shape[0]
    width = hidden.shape[1]
    size = rotated_rollout_keys.shape[2]
    heads_here = queries.shape[1] // size
    group_size = heads_here * members // rotated_rollout_keys.shape[1]
    value_head = member * heads_here // group_size
    scale = math.log2(math.e) / math.sqrt(size)
    heads = 2 * heads_here

    def over(block, axis, route):
        count = lax.axis_size(axis)
        pairs = [(i, route(i)) for i in range(count) if route(i) is not None]
        return lax.ppermute(block, axis, pairs)

    positions = cached_key_slabs.shape[0]
    half = positions // 2

    def half_of(slab):
        cut = slab.reshape(half // BLOCK, 2, BLOCK, slab.shape[1], size)
        cut = lax.dynamic_index_in_dim(cut, core, 1, keepdims=False)
        return lax.dynamic_index_in_dim(cut, value_head, 2, keepdims=False).reshape(half, size)

    line = lax.broadcasted_iota(jnp.int32, (META, size), 0)
    numbers = jnp.where(
        line == 0, piece_offset[0], jnp.where(line == 1, piece_len[0] // 256, piece_len[0] % 256)
    )
    kv = jnp.concatenate(
        [half_of(cached_key_slabs), half_of(cached_value_slabs), numbers.astype(jnp.bfloat16)]
    )
    two = over(kv, "req", lambda i: (i - 2) % groups)
    one = over(kv, "req", lambda i: i - 1 if i % 2 else None)
    mate_queries = over(queries, "mp", lambda i: i ^ 1)
    mate_weight = over(out_weight, "mp", lambda i: i ^ 1)
    swap = over(two, "req", lambda i: i ^ 1)
    three = over(swap, "req", lambda i: (i - 2) % groups if i % 2 else None)

    order = list(range(0, members, 2)) + list(range(1, members, 2))

    def arrange(block):
        return [lax.dynamic_slice_in_dim(block, (member ^ k) * rows_here, rows_here) for k in order]

    query = jnp.concatenate(
        [jnp.concatenate(arrange(part)) for part in (queries, mate_queries)], axis=1
    )
    times = jnp.concatenate(
        [(member ^ k) * rows_here + jnp.arange(rows_here, dtype=jnp.int32) for k in order]
    )[None]

    def own_half(block):
        cut = lax.dynamic_index_in_dim(block, value_head, 1, keepdims=False)
        return lax.dynamic_slice_in_dim(cut, core * (rollout // 2), rollout // 2)

    full = shape((heads, size + STATE, rollout))
    part = shape((heads, size + STATE, rollout // 2))
    numbers = functools.partial(jnp.stack)
    work = 4 * heads * rollout * half * size
    state = call(
        functools.partial(first_kernel, size=size, scale=scale),
        full,
        [smem()] + [vmem()] * 5,
        16,
        work,
        2 * half * size * 4,
    )(
        jnp.stack([core, jnp.zeros_like(core)]),
        times,
        query,
        own_half(rotated_rollout_keys),
        own_half(rollout_value_matrix),
        kv,
    )
    even = request % 2 == 0
    first_tags = jnp.stack([core, jnp.full_like(core, 1), jnp.full_like(core, 2)])
    swap_tags = jnp.stack([core, jnp.where(even, 3, 1)])
    last_tags = jnp.stack([core, jnp.full_like(core, 3)])
    state = call(
        functools.partial(more_kernel, size=size, scale=scale, slots=2, split=False),
        full,
        [smem()] + [vmem()] * 4,
        16,
        2 * work,
        4 * half * size * 4,
    )(first_tags, query, one, two, state)
    state = call(
        functools.partial(more_kernel, size=size, scale=scale, slots=1, split=False),
        full,
        [smem()] + [vmem()] * 3,
        16,
        work,
        2 * half * size * 4,
    )(swap_tags, query, swap, state)
    kept, sent = call(
        functools.partial(more_kernel, size=size, scale=scale, slots=1, split=True),
        (part, part),
        [smem()] + [vmem()] * 3,
        16,
        work,
        2 * half * size * 4,
        scratch_shapes=[pltpu.VMEM(full.shape, jnp.float32)],
    )(last_tags, query, three, state)
    came = over(sent, "mp", lambda i: i ^ 1)

    tile = 1024
    rows_core = rollout // 2
    away = rows_core - rows_here
    own, send = pl.pallas_call(
        functools.partial(merge_kernel, size=size, rows=rows_here),
        out_shape=(shape((rows_here, width)), shape((away, width), jnp.bfloat16)),
        grid=(width // tile,),
        in_specs=[
            pl.BlockSpec(part.shape, lambda i: (0, 0, 0)),
            pl.BlockSpec(part.shape, lambda i: (0, 0, 0)),
            pl.BlockSpec((out_weight.shape[0], tile), lambda i: (0, i)),
            pl.BlockSpec((out_weight.shape[0], tile), lambda i: (0, i)),
        ],
        out_specs=(
            pl.BlockSpec((rows_here, tile), lambda i: (0, i)),
            pl.BlockSpec((away, tile), lambda i: (0, i)),
        ),
        scratch_shapes=[pltpu.VMEM((rows_core, heads * size), jnp.bfloat16)],
        compiler_params=pltpu.CompilerParams(vmem_limit_bytes=16 * MIB),
        cost_estimate=pl.CostEstimate(
            flops=2 * rows_core * heads * size * width,
            bytes_accessed=4 * out_weight.shape[0] * width,
            transcendentals=0,
        ),
    )(kept, came, out_weight, mate_weight)
    parts = []
    for k in range(1, members // 2):
        block = send[(k - 1) * rows_here : k * rows_here]
        parts.append(over(block, "mp", lambda i, k=k: i ^ (2 * k)))
    rows = call(
        norm_kernel,
        shape((rows_here, width + size), jnp.bfloat16),
        [vmem()] * (4 + len(parts)),
        16,
        0,
        rows_here * width * 8,
    )(own, hidden, final_gain[None], token_ids[:, None], *parts)

    ring = ring_order(groups)
    place = {group: at for at, group in enumerate(ring)}

    def ahead(block):
        return over(block, "req", lambda i: ring[(place[i] + 1) % groups])

    def behind(block):
        return over(block, "req", lambda i: ring[(place[i] - 1) % groups])

    vocabulary_here = head_weight.shape[1]
    weight = head_weight.T
    block = 400 if vocabulary_here % 400 == 0 else vocabulary_here
    first_word = (request * vocabulary_here)[None].astype(jnp.int32)

    def statistics(blocks):
        count = sum(part.shape[0] for part in blocks)
        return call(
            functools.partial(logits_kernel, block=block),
            shape((STATE, count)),
            [smem()] + [vmem()] * (len(blocks) + 1),
            10,
            2 * count * width * vocabulary_here,
            2 * width * vocabulary_here,
            scratch_shapes=[
                pltpu.VMEM((count, width), jnp.bfloat16),
                pltpu.VMEM((count, size), jnp.float32),
            ],
        )(first_word, *blocks, weight)

    passed, returned = [rows], [rows]
    for _ in range(groups // 2 - 1):
        passed.append(ahead(passed[-1]))
        returned.append(behind(returned[-1]))
    middle = rows_here // 2
    final = [ahead(passed[-1][:middle]), behind(returned[-1][middle:])]
    arrived = [[rows]] + [[passed[s], returned[s]] for s in range(1, groups // 2)] + [final]
    names = [[0]] + [[-s, s] for s in range(1, groups // 2)] + [[groups // 2]]
    found = {}
    batches = [[0, 1]] + [[s] for s in range(2, groups // 2 - 1)]
    batches += [[groups // 2 - 1, groups // 2]]
    for batch in batches:
        blocks = [part for s in batch for part in arrived[s]]
        table = statistics(blocks)
        at = 0
        for name in [name for s in batch for name in names[s]]:
            found[name % groups] = table[:, at : at + rows_here]
            at += rows_here
    stacked = jnp.stack([found[d] for d in range(groups)])
    where = jnp.array([place[group] for group in range(groups)], jnp.int32)
    stacked = jnp.take(stacked, (where - where[request]) % groups, axis=0)
    pooled = lax.all_to_all(stacked, "req", 0, 0)
    tops = pooled[:, 0]
    highest = jnp.max(tops, axis=0)
    scales = jnp.exp(tops - highest)
    total = jnp.sum(pooled[:, 1] * scales, axis=0)
    weighted = jnp.sum(pooled[:, 2] * scales, axis=0)
    picked = jnp.sum(pooled[:, 3], axis=0)
    log_total = highest + jnp.log(total)
    valid = member * rows_here + jnp.arange(rows_here) < rollout_len[0]
    logprob = jnp.where(valid, picked - log_total, 0.0)
    entropy = jnp.where(valid, log_total - weighted / total, 0.0)
    return (logprob, entropy)


def solution(mesh):
    placed = (
        P(("req", "mp"), None),
        P("req", "mp"),
        P("req", None, None),
        P("req", None, None),
        P("req", None, None),
        P("req", None, None),
        P("mp", None),
        P(),
        P(None, "req"),
        P(("req", "mp")),
        P("req"),
        P("req"),
        P("req"),
    )
    return jax.shard_map(
        body,
        mesh=mesh,
        in_specs=placed,
        out_specs=(P(("req", "mp")), P(("req", "mp"))),
        check_vma=False,
    )
```

```python
import functools
import math

import jax
import jax.numpy as jnp
from jax import lax
from jax.experimental import pallas as pl
from jax.experimental.pallas import tpu as pltpu
from jax.sharding import PartitionSpec as P

NEGATIVE = -1e30
BLOCK = 256
META = 16
STATE = 8
FACTS = 5
MIB = 1 << 20


def ring_order(groups):
    wide = 1 << (int(math.log2(groups)) // 2)
    tall = groups // wide
    order = [z * wide for z in range(tall)]
    for step, z in enumerate(reversed(range(tall))):
        across = range(1, wide) if step % 2 == 0 else reversed(range(1, wide))
        order += [z * wide + x for x in across]
    return order


def nt(a, b):
    return lax.dot_general(a, b, (((1,), (1,)), ((), ())), preferred_element_type=jnp.float32)


def tn(a, b):
    return lax.dot_general(a, b, (((0,), (0,)), ((), ())), preferred_element_type=jnp.float32)


def put_state(state, head, size, top, total):
    rows = lax.broadcasted_iota(jnp.int32, (STATE, top.shape[1]), 0)
    state[head, size : size + STATE, :] = jnp.where(rows == 0, top, total)


def attend_slab(core, want, kv, query, state, size, scale):
    half = (kv.shape[0] - META) // 2
    heads = query.shape[1] // size
    meta = kv[2 * half : 2 * half + META, :].astype(jnp.float32)
    offset = jnp.max(meta[0:1, :]).astype(jnp.int32)
    length = jnp.max(meta[1:2, :] * 256.0 + meta[2:3, :]).astype(jnp.int32)
    blocks = jnp.clip((length - core * BLOCK + 2 * BLOCK - 1) // (2 * BLOCK), 0, half // BLOCK)
    blocks = jnp.where(offset == want, blocks, 0)

    def step(j, carry):
        start = pl.multiple_of(j * BLOCK, BLOCK)
        keys = kv[pl.ds(start, BLOCK), :]
        values = kv[pl.ds(half + start, BLOCK), :]
        place = lax.broadcasted_iota(jnp.int32, (BLOCK, 1), 0) + (2 * j + core) * BLOCK
        valid = place < length
        for h in range(heads):
            scores = nt(keys, query[:, h * size : (h + 1) * size]) * scale
            scores = jnp.where(valid, scores, NEGATIVE)
            before = state[h, size : size + 1, :]
            top = jnp.maximum(before, jnp.max(scores, axis=0, keepdims=True))
            old = jnp.exp2(before - top)
            weights = jnp.exp2(scores - top)
            total = state[h, size + 1 : size + 2, :] * old + jnp.sum(weights, axis=0, keepdims=True)
            state[h, :size, :] = state[h, :size, :] * old + tn(values, weights.astype(jnp.bfloat16))
            put_state(state, h, size, top, total)
        return carry

    lax.fori_loop(0, blocks, step, 0)


def first_kernel(sc, times, query, keys, values, kv, state, *, size, scale):
    core = sc[0]
    here = keys.shape[0]
    place = lax.broadcasted_iota(jnp.int32, (here, 1), 0) + core * here
    valid = place <= times[...]
    for h in range(query.shape[1] // size):
        scores = nt(keys[...], query[:, h * size : (h + 1) * size]) * scale
        scores = jnp.where(valid, scores, NEGATIVE)
        top = jnp.max(scores, axis=0, keepdims=True)
        weights = jnp.exp2(scores - top)
        state[h, :size, :] = tn(values[...], weights.astype(jnp.bfloat16))
        put_state(state, h, size, top, jnp.sum(weights, axis=0, keepdims=True))
    attend_slab(core, 0, kv, query, state, size, scale)


def more_kernel(sc, query, *refs, size, scale, wants, split):
    slots = len(wants)
    kvs, given, outs = refs[:slots], refs[slots], refs[slots + 1 :]
    if split:
        state = outs[2]
    else:
        state = outs[0]
    state[...] = given[...]
    for i, kv in enumerate(kvs):
        attend_slab(sc[0], sc[1] if wants[i] is None else wants[i], kv, query, state, size, scale)
    if split:
        middle = state.shape[2] // 2
        outs[0][...] = state[:, :, :middle]
        outs[1][...] = state[:, :, middle:]


def merge_kernel(kept, came, mine, mate, own, *refs, size, rows):
    sends, mixed = refs[:-1], refs[-1]
    heads = kept.shape[0]

    @pl.when(pl.program_id(0) == 0)
    def _():
        for h in range(heads):
            other = (h + heads // 2) % heads
            first, second = kept[h, size : size + 1, :], came[other, size : size + 1, :]
            top = jnp.maximum(first, second)
            left, right = jnp.exp2(first - top), jnp.exp2(second - top)
            total = kept[h, size + 1 : size + 2, :] * left + came[other, size + 1 : size + 2, :] * right
            value = (kept[h, :size, :] * left + came[other, :size, :] * right) / total
            mixed[:, h * size : (h + 1) * size] = value.T.astype(jnp.bfloat16)

    width = mine.shape[0]
    out = jnp.dot(mixed[:, :width], mine[...], preferred_element_type=jnp.float32)
    out += jnp.dot(mixed[:, width:], mate[...], preferred_element_type=jnp.float32)
    own[...] = out[:rows, :]
    at = rows
    for send in sends:
        send[...] = out[at : at + send.shape[0], :].astype(jnp.bfloat16)
        at += send.shape[0]


def norm_kernel(own, hidden, gain, words, *refs):
    came, out = refs[:-1], refs[-1]
    stream = own[...] + hidden[...].astype(jnp.float32)
    for part in came:
        stream += part[...].astype(jnp.float32)
    width = stream.shape[1]
    square = jnp.sum(stream * stream, axis=1, keepdims=True) * (1.0 / width)
    out[:, :width] = (stream * lax.rsqrt(square + 1e-06) * gain[...]).astype(jnp.bfloat16)
    lane = lax.broadcasted_iota(jnp.int32, (stream.shape[0], out.shape[1] - width), 1)
    code = jnp.where(lane == 0, words[...] >> 8, words[...] & 255)
    out[:, width:] = code.astype(jnp.float32).astype(jnp.bfloat16)


def head_kernel(sc, *refs, block, homes, given):
    parts, weight = refs[: len(homes)], refs[len(homes)]
    table, rows, codes, slots, sems = refs[-5:]
    width = weight.shape[1]
    deep = parts[0].shape[0]
    count = deep * len(homes)
    depth = slots.shape[0]
    steps = weight.shape[0] // block

    def fetch(i):
        start, slot = pl.multiple_of(i * block, 8), lax.rem(i, depth)
        source = weight.at[pl.ds(start, block), :]
        return pltpu.make_async_copy(source, slots.at[slot], sems.at[slot])

    for i in range(min(depth - 1, steps)):
        fetch(i).start()
    for i, part in enumerate(parts):
        rows[i * deep : (i + 1) * deep, :] = part[:, :width]
        codes[i * deep : (i + 1) * deep, :] = part[:, width:].astype(jnp.float32)
    turned = codes[...].T
    words = (turned[0:1, :] * 256.0 + turned[1:2, :]).astype(jnp.int32) - sc[2]
    place = lax.broadcasted_iota(jnp.int32, (block, 1), 0)

    def step(i, carry):
        top, total, weighted, picked = carry
        fetch(i).wait()

        @pl.when(i + depth - 1 < steps)
        def _():
            fetch(i + depth - 1).start()

        logits = nt(slots[lax.rem(i, depth)], rows[...])
        now = jnp.maximum(top, jnp.max(logits, axis=0, keepdims=True))
        old = jnp.exp(top - now)
        spread = jnp.exp(logits - now)
        total = total * old + jnp.sum(spread, axis=0, keepdims=True)
        weighted = weighted * old + jnp.sum(spread * logits, axis=0, keepdims=True)
        hit = place == words - i * block
        picked = picked + jnp.sum(jnp.where(hit, logits, 0.0), axis=0, keepdims=True)
        return now, total, weighted, picked

    zero = jnp.zeros((1, count), jnp.float32)
    carry = (jnp.full((1, count), NEGATIVE, jnp.float32), zero, zero, zero)
    top, total, weighted, picked = lax.fori_loop(0, steps, step, carry)
    line = lax.broadcasted_iota(jnp.int32, (STATE, count), 0)
    value = jnp.where(line == 0, top, jnp.where(line == 1, total, weighted))
    value = jnp.where(line == 3, picked, value)
    if given:
        table[...] = refs[len(homes) + 1][...]
    else:
        table[...] = jnp.zeros_like(table)
    for i, (name, side) in enumerate(homes):
        piece = value[:, i * deep : (i + 1) * deep]
        table[sc[FACTS + name], :, side * deep : (side + 1) * deep] = piece


def final_kernel(sc, pooled, out):
    tops = pooled[:, 0:1, :]
    highest = jnp.max(tops, axis=0)
    scales = jnp.exp(tops - highest[None])
    total = jnp.sum(pooled[:, 1:2, :] * scales, axis=0)
    weighted = jnp.sum(pooled[:, 2:3, :] * scales, axis=0)
    picked = jnp.sum(pooled[:, 3:4, :], axis=0)
    log_total = highest + jnp.log(total)
    place = lax.broadcasted_iota(jnp.int32, (1, pooled.shape[2]), 1) + sc[3]
    valid = place < sc[4]
    line = lax.broadcasted_iota(jnp.int32, (STATE, pooled.shape[2]), 0)
    value = jnp.where(line == 0, picked - log_total, log_total - weighted / total)
    out[...] = jnp.where(valid, value, 0.0)


def smem():
    return pl.BlockSpec(memory_space=pltpu.SMEM)


def vmem():
    return pl.BlockSpec(memory_space=pltpu.VMEM)


def call(kernel, shapes, specs, limit, flops=0, read=0, **extra):
    return pl.pallas_call(
        kernel,
        out_shape=shapes,
        in_specs=specs,
        compiler_params=pltpu.CompilerParams(vmem_limit_bytes=limit * MIB),
        cost_estimate=pl.CostEstimate(flops=flops, bytes_accessed=read, transcendentals=0),
        **extra,
    )


def shape(dims, kind=jnp.float32):
    return jax.ShapeDtypeStruct(dims, kind)


def body(
    hidden,
    queries,
    rotated_rollout_keys,
    rollout_value_matrix,
    cached_key_slabs,
    cached_value_slabs,
    out_weight,
    final_gain,
    head_weight,
    token_ids,
    rollout_len,
    piece_offset,
    piece_len,
):
    groups, members = lax.axis_size("req"), lax.axis_size("mp")
    request, member = lax.axis_index("req"), lax.axis_index("mp")
    core = member % 2
    rollout, rows_here = queries.shape[0], hidden.shape[0]
    width = hidden.shape[1]
    size = rotated_rollout_keys.shape[2]
    heads_here = queries.shape[1] // size
    group_size = heads_here * members // rotated_rollout_keys.shape[1]
    value_head = member * heads_here // group_size
    scale = math.log2(math.e) / math.sqrt(size)
    heads = 2 * heads_here

    def over(block, axis, route):
        count = lax.axis_size(axis)
        pairs = [(i, route(i)) for i in range(count) if route(i) is not None]
        return lax.ppermute(block, axis, pairs)

    positions = cached_key_slabs.shape[0]
    half = positions // 2

    def half_of(slab):
        cut = slab.reshape(half // BLOCK, 2, BLOCK, slab.shape[1], size)
        cut = lax.dynamic_index_in_dim(cut, core, 1, keepdims=False)
        return lax.dynamic_index_in_dim(cut, value_head, 2, keepdims=False).reshape(half, size)

    line = lax.broadcasted_iota(jnp.int32, (META, size), 0)
    numbers = jnp.where(
        line == 0, piece_offset[0], jnp.where(line == 1, piece_len[0] // 256, piece_len[0] % 256)
    )
    kv = jnp.concatenate(
        [half_of(cached_key_slabs), half_of(cached_value_slabs), numbers.astype(jnp.bfloat16)]
    )
    two = over(kv, "req", lambda i: (i - 2) % groups)
    one = over(kv, "req", lambda i: i - 1 if i % 2 else None)
    mate_queries = over(queries, "mp", lambda i: i ^ 1)
    mate_weight = over(out_weight, "mp", lambda i: i ^ 1)

    vocabulary_here = head_weight.shape[1]
    tour = jnp.array(ring_order(groups), jnp.int32)
    at = jnp.sum(jnp.where(tour == request, jnp.arange(groups, dtype=jnp.int32), 0))
    spots = (at + jnp.arange(groups, dtype=jnp.int32)) % groups
    match = spots[:, None] == jnp.arange(groups, dtype=jnp.int32)[None]
    homes = jnp.sum(jnp.where(match, tour[None], 0), axis=1)
    facts = [core, 3 - 2 * (request % 2), request * vocabulary_here, member * rows_here, rollout_len[0]]
    plan = jnp.concatenate([jnp.stack(facts).astype(jnp.int32), homes])

    order = list(range(0, members, 2)) + list(range(1, members, 2))

    def arrange(block):
        return [lax.dynamic_slice_in_dim(block, (member ^ k) * rows_here, rows_here) for k in order]

    query = jnp.concatenate(
        [jnp.concatenate(arrange(part)) for part in (queries, mate_queries)], axis=1
    )
    times = jnp.concatenate(
        [(member ^ k) * rows_here + jnp.arange(rows_here, dtype=jnp.int32) for k in order]
    )[None]

    def own_half(block):
        cut = lax.dynamic_index_in_dim(block, value_head, 1, keepdims=False)
        return lax.dynamic_slice_in_dim(cut, core * (rollout // 2), rollout // 2)

    full = shape((heads, size + STATE, rollout))
    part = shape((heads, size + STATE, rollout // 2))
    work = 4 * heads * rollout * half * size
    state = call(
        functools.partial(first_kernel, size=size, scale=scale),
        full,
        [smem()] + [vmem()] * 5,
        16,
        work,
        2 * half * size * 4,
    )(
        plan,
        times,
        query,
        own_half(rotated_rollout_keys),
        own_half(rollout_value_matrix),
        kv,
    )
    two, state = lax.optimization_barrier((two, state))
    swap = over(two, "req", lambda i: i ^ 1)
    state = call(
        functools.partial(more_kernel, size=size, scale=scale, wants=(1, 2), split=False),
        full,
        [smem()] + [vmem()] * 4,
        16,
        2 * work,
        4 * half * size * 4,
    )(plan, query, one, two, state)
    swap, state = lax.optimization_barrier((swap, state))
    three = over(swap, "req", lambda i: (i - 2) % groups if i % 2 else None)
    state = call(
        functools.partial(more_kernel, size=size, scale=scale, wants=(None,), split=False),
        full,
        [smem()] + [vmem()] * 3,
        16,
        work,
        2 * half * size * 4,
    )(plan, query, swap, state)
    kept, sent = call(
        functools.partial(more_kernel, size=size, scale=scale, wants=(3,), split=True),
        (part, part),
        [smem()] + [vmem()] * 3,
        16,
        work,
        2 * half * size * 4,
        scratch_shapes=[pltpu.VMEM(full.shape, jnp.float32)],
    )(plan, query, three, state)
    came = over(sent, "mp", lambda i: i ^ 1)

    tile = 1024
    rows_core = rollout // 2
    deep = rows_here // 2
    pieces = [(k, side) for k in range(1, members // 2) for side in (0, 1)]
    own, *sends = pl.pallas_call(
        functools.partial(merge_kernel, size=size, rows=rows_here),
        out_shape=(shape((rows_here, width)), *[shape((deep, width), jnp.bfloat16)] * len(pieces)),
        grid=(width // tile,),
        in_specs=[
            pl.BlockSpec(part.shape, lambda i: (0, 0, 0)),
            pl.BlockSpec(part.shape, lambda i: (0, 0, 0)),
            pl.BlockSpec((out_weight.shape[0], tile), lambda i: (0, i)),
            pl.BlockSpec((out_weight.shape[0], tile), lambda i: (0, i)),
        ],
        out_specs=(
            pl.BlockSpec((rows_here, tile), lambda i: (0, i)),
            *[pl.BlockSpec((deep, tile), lambda i: (0, i))] * len(pieces),
        ),
        scratch_shapes=[pltpu.VMEM((rows_core, heads * size), jnp.bfloat16)],
        compiler_params=pltpu.CompilerParams(vmem_limit_bytes=16 * MIB),
        cost_estimate=pl.CostEstimate(
            flops=2 * rows_core * heads * size * width,
            bytes_accessed=4 * out_weight.shape[0] * width,
            transcendentals=0,
        ),
    )(kept, came, out_weight, mate_weight)

    ring = ring_order(groups)
    place = {group: at for at, group in enumerate(ring)}

    def ahead(block):
        return over(block, "req", lambda i: ring[(place[i] + 1) % groups])

    def behind(block):
        return over(block, "req", lambda i: ring[(place[i] - 1) % groups])

    def normed(side):
        came = [
            over(block, "mp", lambda i, k=k: i ^ (2 * k))
            for (k, half_side), block in zip(pieces, sends)
            if half_side == side
        ]

        def cut(columns):
            return pl.BlockSpec((deep, columns), lambda i: (side, 0))

        return pl.pallas_call(
            norm_kernel,
            out_shape=shape((deep, width + size), jnp.bfloat16),
            grid=(1,),
            in_specs=[cut(width), cut(width), pl.BlockSpec((1, width), lambda i: (0, 0)), cut(1)]
            + [pl.BlockSpec((deep, width), lambda i: (0, 0))] * len(came),
            out_specs=pl.BlockSpec((deep, width + size), lambda i: (0, 0)),
            compiler_params=pltpu.CompilerParams(vmem_limit_bytes=8 * MIB),
            cost_estimate=pl.CostEstimate(
                flops=0, bytes_accessed=deep * width * 8, transcendentals=0
            ),
        )(own, hidden, final_gain[None], token_ids[:, None], *came)

    weight = head_weight.T
    block = 400 if vocabulary_here % 400 == 0 else vocabulary_here
    forth, back = [None, None], [None, None]
    ready = [[], []]
    for side in (0, 1):
        forth[side] = back[side] = normed(side)
        ready[side].append((0, side, forth[side]))
    for step in range(1, groups // 2):
        for side in (0, 1):
            forth[side], back[side] = ahead(forth[side]), behind(back[side])
            ready[side] += [(-step % groups, side, forth[side]), (step, side, back[side])]
    final = [(groups // 2, 0, ahead(forth[0])), (groups // 2, 1, behind(back[1]))]
    own_rows, *_ = lax.optimization_barrier((ready[0][0][2], forth[1], back[1]))
    ready[0][0] = (0, 0, own_rows)
    arrived = ready[0] + ready[1] + final
    batch = max(1, 256 // deep)
    depth = 4
    table = None
    for at in range(0, len(arrived), batch):
        now = arrived[at : at + batch]
        count = deep * len(now)
        given = [] if table is None else [table]
        table = call(
            functools.partial(
                head_kernel,
                block=block,
                homes=[(name, side) for name, side, _ in now],
                given=len(given),
            ),
            shape((groups, STATE, 128)),
            [smem()]
            + [vmem()] * len(now)
            + [pl.BlockSpec(memory_space=pl.ANY)]
            + [vmem()] * len(given),
            44,
            2 * count * width * vocabulary_here,
            2 * width * vocabulary_here,
            scratch_shapes=[
                pltpu.VMEM((count, width), jnp.bfloat16),
                pltpu.VMEM((count, size), jnp.float32),
                pltpu.VMEM((depth, block, width), jnp.bfloat16),
                pltpu.SemaphoreType.DMA((depth,)),
            ],
        )(plan, *[rows for _, _, rows in now], weight, *given)
    pooled = lax.all_to_all(table, "req", 0, 0)
    out = call(final_kernel, shape((STATE, 128)), [smem(), vmem()], 4)(plan, pooled)
    return (out[0, :rows_here], out[1, :rows_here])


def solution(mesh):
    placed = (
        P(("req", "mp"), None),
        P("req", "mp"),
        P("req", None, None),
        P("req", None, None),
        P("req", None, None),
        P("req", None, None),
        P("mp", None),
        P(),
        P(None, "req"),
        P(("req", "mp")),
        P("req"),
        P("req"),
        P("req"),
    )
    return jax.shard_map(
        body,
        mesh=mesh,
        in_specs=placed,
        out_specs=(P(("req", "mp")), P(("req", "mp"))),
        check_vma=False,
    )
```

```python
import functools
import math

import jax
import jax.numpy as jnp
from jax import lax
from jax.experimental import pallas as pl
from jax.experimental.pallas import tpu as pltpu
from jax.sharding import PartitionSpec as P

NEGATIVE = -1e30
BLOCK = 256
META = 16
STATE = 8
FACTS = 5
PARTS = 2
MIB = 1 << 20


def ring_order(groups):
    wide = 1 << (int(math.log2(groups)) // 2)
    tall = groups // wide
    order = [z * wide for z in range(tall)]
    for step, z in enumerate(reversed(range(tall))):
        across = range(1, wide) if step % 2 == 0 else reversed(range(1, wide))
        order += [z * wide + x for x in across]
    return order


def nt(a, b):
    return lax.dot_general(a, b, (((1,), (1,)), ((), ())), preferred_element_type=jnp.float32)


def tn(a, b):
    return lax.dot_general(a, b, (((0,), (0,)), ((), ())), preferred_element_type=jnp.float32)


def put_state(state, head, size, top, total):
    rows = lax.broadcasted_iota(jnp.int32, (STATE, top.shape[1]), 0)
    state[head, size : size + STATE, :] = jnp.where(rows == 0, top, total)


def attend_slab(core, want, part, kv, query, state, size, scale):
    half = (kv.shape[0] - META) // 2
    heads = query.shape[1] // size
    meta = kv[2 * half : 2 * half + META, :].astype(jnp.float32)
    offset = jnp.max(meta[0:1, :]).astype(jnp.int32)
    length = jnp.max(meta[1:2, :] * 256.0 + meta[2:3, :]).astype(jnp.int32)
    begin = part * half
    blocks = (length - core * BLOCK + 2 * BLOCK - 1) // (2 * BLOCK)
    blocks = jnp.clip(blocks - begin // BLOCK, 0, half // BLOCK)
    blocks = jnp.where(offset == want, (blocks + 1) // 2, 0)
    wide = 2 * BLOCK

    def step(j, carry):
        start = pl.multiple_of(j * wide, wide)
        keys = kv[pl.ds(start, wide), :]
        values = kv[pl.ds(half + start, wide), :]
        local = lax.broadcasted_iota(jnp.int32, (wide, 1), 0) + (start + begin)
        place = (local // BLOCK) * (2 * BLOCK) + core * BLOCK + local % BLOCK
        bias = jnp.where(place < length, 0.0, NEGATIVE)
        products = [nt(keys, query[:, h * size : (h + 1) * size]) for h in range(heads)]
        for h in range(heads):
            scores = products[h] * scale + bias
            before = state[h, size : size + 1, :]
            top = jnp.maximum(before, jnp.max(scores, axis=0, keepdims=True))
            old = jnp.exp2(before - top)
            weights = jnp.exp2(scores - top)
            total = state[h, size + 1 : size + 2, :] * old + jnp.sum(weights, axis=0, keepdims=True)
            state[h, :size, :] = state[h, :size, :] * old + tn(values, weights.astype(jnp.bfloat16))
            put_state(state, h, size, top, total)
        return carry

    lax.fori_loop(0, blocks, step, 0)


def first_kernel(sc, times, query, keys, values, *refs, size, scale):
    kvs, state = refs[:-1], refs[-1]
    core = sc[0]
    here = keys.shape[0]
    place = lax.broadcasted_iota(jnp.int32, (here, 1), 0) + core * here
    valid = place <= times[...]
    heads = query.shape[1] // size
    products = [nt(keys[...], query[:, h * size : (h + 1) * size]) for h in range(heads)]
    for h in range(heads):
        scores = jnp.where(valid, products[h] * scale, NEGATIVE)
        top = jnp.max(scores, axis=0, keepdims=True)
        weights = jnp.exp2(scores - top)
        state[h, :size, :] = tn(values[...], weights.astype(jnp.bfloat16))
        put_state(state, h, size, top, jnp.sum(weights, axis=0, keepdims=True))
    for part, kv in enumerate(kvs):
        attend_slab(core, 0, part, kv, query, state, size, scale)


def more_kernel(sc, query, *refs, size, scale, wants, split):
    slots = len(wants)
    kvs, given, outs = refs[:slots], refs[slots], refs[slots + 1 :]
    if split:
        state = outs[2]
    else:
        state = outs[0]
    state[...] = given[...]
    for i, kv in enumerate(kvs):
        want = sc[1] if wants[i] is None else wants[i]
        attend_slab(sc[0], want, i % PARTS, kv, query, state, size, scale)
    if split:
        middle = state.shape[2] // 2
        outs[0][...] = state[:, :, :middle]
        outs[1][...] = state[:, :, middle:]


def merge_kernel(kept, came, mine, mate, own, *refs, size, rows):
    sends, mixed = refs[:-1], refs[-1]
    heads = kept.shape[0]

    @pl.when(pl.program_id(0) == 0)
    def _():
        for h in range(heads):
            other = (h + heads // 2) % heads
            first, second = kept[h, size : size + 1, :], came[other, size : size + 1, :]
            top = jnp.maximum(first, second)
            left, right = jnp.exp2(first - top), jnp.exp2(second - top)
            total = kept[h, size + 1 : size + 2, :] * left + came[other, size + 1 : size + 2, :] * right
            value = (kept[h, :size, :] * left + came[other, :size, :] * right) / total
            mixed[:, h * size : (h + 1) * size] = value.T.astype(jnp.bfloat16)

    width = mine.shape[0]
    out = jnp.dot(mixed[:, :width], mine[...], preferred_element_type=jnp.float32)
    out += jnp.dot(mixed[:, width:], mate[...], preferred_element_type=jnp.float32)
    own[...] = out[:rows, :]
    at = rows
    for send in sends:
        send[...] = out[at : at + send.shape[0], :].astype(jnp.bfloat16)
        at += send.shape[0]


def norm_kernel(own, hidden, gain, words, *refs):
    came, out = refs[:-1], refs[-1]
    stream = own[...] + hidden[...].astype(jnp.float32)
    for part in came:
        stream += part[...].astype(jnp.float32)
    width = stream.shape[1]
    square = jnp.sum(stream * stream, axis=1, keepdims=True) * (1.0 / width)
    out[:, :width] = (stream * lax.rsqrt(square + 1e-06) * gain[...]).astype(jnp.bfloat16)
    lane = lax.broadcasted_iota(jnp.int32, (stream.shape[0], out.shape[1] - width), 1)
    code = jnp.where(lane == 0, words[...] >> 8, words[...] & 255)
    out[:, width:] = code.astype(jnp.float32).astype(jnp.bfloat16)


def head_kernel(sc, *refs, block, homes, given, finish):
    parts, weight = refs[: len(homes)], refs[len(homes)]
    table, rows, codes, slots, sems = refs[-5:]
    width = weight.shape[1]
    deep = parts[0].shape[0]
    count = deep * len(homes)
    depth = slots.shape[0]
    steps = weight.shape[0] // block

    def fetch(i):
        start, slot = pl.multiple_of(i * block, 8), lax.rem(i, depth)
        source = weight.at[pl.ds(start, block), :]
        return pltpu.make_async_copy(source, slots.at[slot], sems.at[slot])

    for i in range(min(depth - 1, steps)):
        fetch(i).start()
    for i, part in enumerate(parts):
        rows[i * deep : (i + 1) * deep, :] = part[:, :width]
        codes[i * deep : (i + 1) * deep, :] = part[:, width:].astype(jnp.float32)
    turned = codes[...].T
    words = (turned[0:1, :] * 256.0 + turned[1:2, :]).astype(jnp.int32) - sc[2]
    place = lax.broadcasted_iota(jnp.int32, (block, 1), 0)

    def step(i, carry):
        top, total, weighted, picked = carry
        fetch(i).wait()

        @pl.when(i + depth - 1 < steps)
        def _():
            fetch(i + depth - 1).start()

        logits = nt(slots[lax.rem(i, depth)], rows[...])
        now = jnp.maximum(top, jnp.max(logits, axis=0, keepdims=True))
        old = jnp.exp(top - now)
        spread = jnp.exp(logits - now)
        total = total * old + jnp.sum(spread, axis=0, keepdims=True)
        weighted = weighted * old + jnp.sum(spread * logits, axis=0, keepdims=True)
        hit = place == words - i * block
        picked = picked + jnp.sum(jnp.where(hit, logits, 0.0), axis=0, keepdims=True)
        return now, total, weighted, picked

    zero = jnp.zeros((1, count), jnp.float32)
    carry = (jnp.full((1, count), NEGATIVE, jnp.float32), zero, zero, zero)
    top, total, weighted, picked = lax.fori_loop(0, steps, step, carry)
    line = lax.broadcasted_iota(jnp.int32, (STATE, count), 0)
    value = jnp.where(line == 0, top, jnp.where(line == 1, total, weighted))
    value = jnp.where(line == 3, picked, value)
    held = jnp.zeros(table.shape, jnp.float32) if not given else refs[len(homes) + 1][...]
    table[...] = held
    for i, (name, side) in enumerate(homes):
        piece = value[:, i * deep : (i + 1) * deep]
        table[sc[FACTS + name], :, side * deep : (side + 1) * deep] = piece
    if finish:
        low, high = refs[-7:-5]
        low[...] = table[: low.shape[0]]
        high[...] = table[low.shape[0] :]


def joined(mine, other):
    highest = jnp.maximum(mine[:, 0:1, :], other[:, 0:1, :])
    left, right = jnp.exp(mine[:, 0:1, :] - highest), jnp.exp(other[:, 0:1, :] - highest)
    line = lax.broadcasted_iota(jnp.int32, mine.shape, 1)
    scaled = mine * left + other * right
    return jnp.where(line == 0, highest, jnp.where(line == 3, mine + other, scaled))


def join_kernel(mine, other, low, high):
    both = joined(mine[...], other[...])
    low[...] = both[: low.shape[0]]
    high[...] = both[low.shape[0] :]


def final_kernel(sc, mine, other, logprob, entropy):
    both = joined(mine[...], other[...])[0]
    log_total = both[0:1] + jnp.log(both[1:2])
    place = lax.broadcasted_iota(jnp.int32, (1, both.shape[1]), 1) + sc[3]
    valid = place < sc[4]
    count = logprob.shape[1]
    logprob[...] = jnp.where(valid, both[3:4] - log_total, 0.0)[:, :count]
    entropy[...] = jnp.where(valid, log_total - both[2:3] / both[1:2], 0.0)[:, :count]


def smem():
    return pl.BlockSpec(memory_space=pltpu.SMEM)


def vmem():
    return pl.BlockSpec(memory_space=pltpu.VMEM)


def call(kernel, shapes, specs, limit, flops=0, read=0, **extra):
    return pl.pallas_call(
        kernel,
        out_shape=shapes,
        in_specs=specs,
        compiler_params=pltpu.CompilerParams(vmem_limit_bytes=limit * MIB),
        cost_estimate=pl.CostEstimate(flops=flops, bytes_accessed=read, transcendentals=0),
        **extra,
    )


def shape(dims, kind=jnp.float32):
    return jax.ShapeDtypeStruct(dims, kind)


def body(
    hidden,
    queries,
    rotated_rollout_keys,
    rollout_value_matrix,
    cached_key_slabs,
    cached_value_slabs,
    out_weight,
    final_gain,
    head_weight,
    token_ids,
    rollout_len,
    piece_offset,
    piece_len,
):
    groups, members = lax.axis_size("req"), lax.axis_size("mp")
    request, member = lax.axis_index("req"), lax.axis_index("mp")
    core = member % 2
    rollout, rows_here = queries.shape[0], hidden.shape[0]
    width = hidden.shape[1]
    size = rotated_rollout_keys.shape[2]
    heads_here = queries.shape[1] // size
    group_size = heads_here * members // rotated_rollout_keys.shape[1]
    value_head = member * heads_here // group_size
    scale = math.log2(math.e) / math.sqrt(size)
    heads = 2 * heads_here

    def over(block, axis, route):
        count = lax.axis_size(axis)
        pairs = [(i, route(i)) for i in range(count) if route(i) is not None]
        return lax.ppermute(block, axis, pairs)

    positions = cached_key_slabs.shape[0]
    half = positions // 2

    def half_of(slab):
        cut = slab.reshape(half // BLOCK, 2, BLOCK, slab.shape[1], size)
        cut = lax.dynamic_index_in_dim(cut, core, 1, keepdims=False)
        return lax.dynamic_index_in_dim(cut, value_head, 2, keepdims=False).reshape(half, size)

    line = lax.broadcasted_iota(jnp.int32, (META, size), 0)
    numbers = jnp.where(
        line == 0, piece_offset[0], jnp.where(line == 1, piece_len[0] // 256, piece_len[0] % 256)
    )
    all_keys, all_values = half_of(cached_key_slabs), half_of(cached_value_slabs)
    deep = half // PARTS
    kv = [
        jnp.concatenate(
            [
                all_keys[p * deep : (p + 1) * deep],
                all_values[p * deep : (p + 1) * deep],
                numbers.astype(jnp.bfloat16),
            ]
        )
        for p in range(PARTS)
    ]
    two = [over(part, "req", lambda i: (i - 2) % groups) for part in kv]
    one = [over(part, "req", lambda i: i - 1 if i % 2 else None) for part in kv]
    mate_queries = over(queries, "mp", lambda i: i ^ 1)
    mate_weight = over(out_weight, "mp", lambda i: i ^ 1)

    vocabulary_here = head_weight.shape[1]
    tour = jnp.array(ring_order(groups), jnp.int32)
    at = jnp.sum(jnp.where(tour == request, jnp.arange(groups, dtype=jnp.int32), 0))
    spots = (at + jnp.arange(groups, dtype=jnp.int32)) % groups
    match = spots[:, None] == jnp.arange(groups, dtype=jnp.int32)[None]
    homes = jnp.sum(jnp.where(match, tour[None], 0), axis=1) ^ request
    facts = [core, 3 - 2 * (request % 2), request * vocabulary_here, member * rows_here, rollout_len[0]]
    plan = jnp.concatenate([jnp.stack(facts).astype(jnp.int32), homes])

    order = list(range(0, members, 2)) + list(range(1, members, 2))

    def arrange(block):
        return [lax.dynamic_slice_in_dim(block, (member ^ k) * rows_here, rows_here) for k in order]

    query = jnp.concatenate(
        [jnp.concatenate(arrange(part)) for part in (queries, mate_queries)], axis=1
    )
    times = jnp.concatenate(
        [(member ^ k) * rows_here + jnp.arange(rows_here, dtype=jnp.int32) for k in order]
    )[None]

    def own_half(block):
        cut = lax.dynamic_index_in_dim(block, value_head, 1, keepdims=False)
        return lax.dynamic_slice_in_dim(cut, core * (rollout // 2), rollout // 2)

    full = shape((heads, size + STATE, rollout))
    part = shape((heads, size + STATE, rollout // 2))
    work = 4 * heads * rollout * half * size
    state = call(
        functools.partial(first_kernel, size=size, scale=scale),
        full,
        [smem()] + [vmem()] * (4 + PARTS),
        32,
        work,
        2 * half * size * 4,
    )(
        plan,
        times,
        query,
        own_half(rotated_rollout_keys),
        own_half(rollout_value_matrix),
        *kv,
    )
    first_two, state = lax.optimization_barrier((two[0], state))
    second_two, one = lax.optimization_barrier((two[1:], one))
    swap = [over(part, "req", lambda i: i ^ 1) for part in (first_two, *second_two)]
    three = [over(part, "req", lambda i: (i - 2) % groups if i % 2 else None) for part in swap]
    state = call(
        functools.partial(more_kernel, size=size, scale=scale, wants=(1,) * PARTS + (2,) * PARTS, split=False),
        full,
        [smem()] + [vmem()] * (2 + 2 * PARTS),
        32,
        2 * work,
        4 * half * size * 4,
    )(plan, query, *one, *two, state)
    state = call(
        functools.partial(more_kernel, size=size, scale=scale, wants=(None,) * PARTS, split=False),
        full,
        [smem()] + [vmem()] * (2 + PARTS),
        32,
        work,
        2 * half * size * 4,
    )(plan, query, *swap, state)
    kept, sent = call(
        functools.partial(more_kernel, size=size, scale=scale, wants=(3,) * PARTS, split=True),
        (part, part),
        [smem()] + [vmem()] * (2 + PARTS),
        32,
        work,
        2 * half * size * 4,
        scratch_shapes=[pltpu.VMEM(full.shape, jnp.float32)],
    )(plan, query, *three, state)
    came = over(sent, "mp", lambda i: i ^ 1)

    tile = 1024
    rows_core = rollout // 2
    deep = rows_here // 2
    pieces = [(k, side) for k in range(1, members // 2) for side in (0, 1)]
    own, *sends = pl.pallas_call(
        functools.partial(merge_kernel, size=size, rows=rows_here),
        out_shape=(shape((rows_here, width)), *[shape((deep, width), jnp.bfloat16)] * len(pieces)),
        grid=(width // tile,),
        in_specs=[
            pl.BlockSpec(part.shape, lambda i: (0, 0, 0)),
            pl.BlockSpec(part.shape, lambda i: (0, 0, 0)),
            pl.BlockSpec((out_weight.shape[0], tile), lambda i: (0, i)),
            pl.BlockSpec((out_weight.shape[0], tile), lambda i: (0, i)),
        ],
        out_specs=(
            pl.BlockSpec((rows_here, tile), lambda i: (0, i)),
            *[pl.BlockSpec((deep, tile), lambda i: (0, i))] * len(pieces),
        ),
        scratch_shapes=[pltpu.VMEM((rows_core, heads * size), jnp.bfloat16)],
        compiler_params=pltpu.CompilerParams(vmem_limit_bytes=16 * MIB),
        cost_estimate=pl.CostEstimate(
            flops=2 * rows_core * heads * size * width,
            bytes_accessed=4 * out_weight.shape[0] * width,
            transcendentals=0,
        ),
    )(kept, came, out_weight, mate_weight)

    ring = ring_order(groups)
    place = {group: at for at, group in enumerate(ring)}

    def ahead(block):
        return over(block, "req", lambda i: ring[(place[i] + 1) % groups])

    def behind(block):
        return over(block, "req", lambda i: ring[(place[i] - 1) % groups])

    def normed(side):
        came = [
            over(block, "mp", lambda i, k=k: i ^ (2 * k))
            for (k, half_side), block in zip(pieces, sends)
            if half_side == side
        ]

        def cut(columns):
            return pl.BlockSpec((deep, columns), lambda i: (side, 0))

        return pl.pallas_call(
            norm_kernel,
            out_shape=shape((deep, width + size), jnp.bfloat16),
            grid=(1,),
            in_specs=[cut(width), cut(width), pl.BlockSpec((1, width), lambda i: (0, 0)), cut(1)]
            + [pl.BlockSpec((deep, width), lambda i: (0, 0))] * len(came),
            out_specs=pl.BlockSpec((deep, width + size), lambda i: (0, 0)),
            compiler_params=pltpu.CompilerParams(vmem_limit_bytes=8 * MIB),
            cost_estimate=pl.CostEstimate(
                flops=0, bytes_accessed=deep * width * 8, transcendentals=0
            ),
        )(own, hidden, final_gain[None], token_ids[:, None], *came)

    weight = head_weight.T
    block = 400 if vocabulary_here % 400 == 0 else vocabulary_here
    forth, back = [None, None], [None, None]
    ready = [[], []]
    for side in (0, 1):
        forth[side] = back[side] = normed(side)
        ready[side].append((0, side, forth[side]))
    for step in range(1, groups // 2):
        for side in (0, 1):
            forth[side], back[side] = ahead(forth[side]), behind(back[side])
            ready[side] += [(-step % groups, side, forth[side]), (step, side, back[side])]
    final = [(groups // 2, 0, ahead(forth[0])), (groups // 2, 1, behind(back[1]))]
    own_rows, *_ = lax.optimization_barrier((ready[0][0][2], forth[1], back[1]))
    ready[0][0] = (0, 0, own_rows)
    arrived = ready[0] + ready[1] + final
    batch = max(1, 256 // deep)
    depth = 4
    table = None
    whole, halves = shape((groups, STATE, 128)), shape((groups // 2, STATE, 128))
    for at in range(0, len(arrived), batch):
        now = arrived[at : at + batch]
        count = deep * len(now)
        given = [] if table is None else [table]
        done = at + batch >= len(arrived)
        table = call(
            functools.partial(
                head_kernel,
                block=block,
                homes=[(name, side) for name, side, _ in now],
                given=len(given),
                finish=done,
            ),
            (halves, halves) if done else whole,
            [smem()]
            + [vmem()] * len(now)
            + [pl.BlockSpec(memory_space=pl.ANY)]
            + [vmem()] * len(given),
            44,
            2 * count * width * vocabulary_here,
            2 * width * vocabulary_here,
            scratch_shapes=[pltpu.VMEM(whole.shape, jnp.float32)] * done
            + [
                pltpu.VMEM((count, width), jnp.bfloat16),
                pltpu.VMEM((count, size), jnp.float32),
                pltpu.VMEM((depth, block, width), jnp.bfloat16),
                pltpu.SemaphoreType.DMA((depth,)),
            ],
        )(plan, *[rows for _, _, rows in now], weight, *given)
    mine, away = table
    bit = groups // 2
    while bit > 1:
        other = over(away, "req", lambda i, bit=bit: i ^ bit)
        bit //= 2
        part = shape((bit, STATE, 128))
        mine, away = call(join_kernel, (part, part), [vmem()] * 2, 4)(mine, other)
    other = over(away, "req", lambda i: i ^ 1)
    rows_out = shape((1, rows_here))
    logprob, entropy = call(final_kernel, (rows_out, rows_out), [smem()] + [vmem()] * 2, 4)(
        plan, mine, other
    )
    return (logprob.reshape(rows_here), entropy.reshape(rows_here))


def solution(mesh):
    placed = (
        P(("req", "mp"), None),
        P("req", "mp"),
        P("req", None, None),
        P("req", None, None),
        P("req", None, None),
        P("req", None, None),
        P("mp", None),
        P(),
        P(None, "req"),
        P(("req", "mp")),
        P("req"),
        P("req"),
        P("req"),
    )
    return jax.shard_map(
        body,
        mesh=mesh,
        in_specs=placed,
        out_specs=(P(("req", "mp")), P(("req", "mp"))),
        check_vma=False,
    )
```

```python
import functools
import math

import jax
import jax.numpy as jnp
from jax import lax
from jax.experimental import pallas as pl
from jax.experimental.pallas import tpu as pltpu
from jax.sharding import PartitionSpec as P

NEGATIVE = -1e30
BLOCK = 256
META = 16
STATE = 8
FACTS = 5
PARTS = 2
MIB = 1 << 20


def ring_order(groups):
    wide = 1 << (int(math.log2(groups)) // 2)
    tall = groups // wide
    order = [z * wide for z in range(tall)]
    for step, z in enumerate(reversed(range(tall))):
        across = range(1, wide) if step % 2 == 0 else reversed(range(1, wide))
        order += [z * wide + x for x in across]
    return order


def nt(a, b):
    return lax.dot_general(a, b, (((1,), (1,)), ((), ())), preferred_element_type=jnp.float32)


def tn(a, b):
    return lax.dot_general(a, b, (((0,), (0,)), ((), ())), preferred_element_type=jnp.float32)


def put_state(state, head, size, top, total):
    rows = lax.broadcasted_iota(jnp.int32, (STATE, top.shape[1]), 0)
    state[head, size : size + STATE, :] = jnp.where(rows == 0, top, total)


def attend_slab(core, want, part, kv, query, state, size, scale):
    half = (kv.shape[0] - META) // 2
    heads = query.shape[1] // size
    meta = kv[2 * half : 2 * half + META, :].astype(jnp.float32)
    offset = jnp.max(meta[0:1, :]).astype(jnp.int32)
    length = jnp.max(meta[1:2, :] * 256.0 + meta[2:3, :]).astype(jnp.int32)
    begin = part * half
    blocks = (length - core * BLOCK + 2 * BLOCK - 1) // (2 * BLOCK)
    blocks = jnp.clip(blocks - begin // BLOCK, 0, half // BLOCK)
    blocks = jnp.where(offset == want, (blocks + 1) // 2, 0)
    wide = 2 * BLOCK

    def step(j, carry):
        start = pl.multiple_of(j * wide, wide)
        keys = kv[pl.ds(start, wide), :]
        values = kv[pl.ds(half + start, wide), :]
        local = lax.broadcasted_iota(jnp.int32, (wide, 1), 0) + (start + begin)
        place = (local // BLOCK) * (2 * BLOCK) + core * BLOCK + local % BLOCK
        bias = jnp.where(place < length, 0.0, NEGATIVE)
        products = [nt(keys, query[:, h * size : (h + 1) * size]) for h in range(heads)]
        for h in range(heads):
            scores = products[h] * scale + bias
            before = state[h, size : size + 1, :]
            top = jnp.maximum(before, jnp.max(scores, axis=0, keepdims=True))
            old = jnp.exp2(before - top)
            weights = jnp.exp2(scores - top)
            total = state[h, size + 1 : size + 2, :] * old + jnp.sum(weights, axis=0, keepdims=True)
            state[h, :size, :] = state[h, :size, :] * old + tn(values, weights.astype(jnp.bfloat16))
            put_state(state, h, size, top, total)
        return carry

    lax.fori_loop(0, blocks, step, 0)


def first_kernel(sc, times, query, keys, values, *refs, size, scale):
    kvs, state = refs[:-1], refs[-1]
    core = sc[0]
    here = keys.shape[0]
    place = lax.broadcasted_iota(jnp.int32, (here, 1), 0) + core * here
    valid = place <= times[...]
    heads = query.shape[1] // size
    products = [nt(keys[...], query[:, h * size : (h + 1) * size]) for h in range(heads)]
    for h in range(heads):
        scores = jnp.where(valid, products[h] * scale, NEGATIVE)
        top = jnp.max(scores, axis=0, keepdims=True)
        weights = jnp.exp2(scores - top)
        state[h, :size, :] = tn(values[...], weights.astype(jnp.bfloat16))
        put_state(state, h, size, top, jnp.sum(weights, axis=0, keepdims=True))
    for part, kv in enumerate(kvs):
        attend_slab(core, 0, part, kv, query, state, size, scale)


def more_kernel(sc, query, *refs, size, scale, wants, split):
    slots = len(wants)
    kvs, given, outs = refs[:slots], refs[slots], refs[slots + 1 :]
    if split:
        state = outs[2]
    else:
        state = outs[0]
    state[...] = given[...]
    for i, kv in enumerate(kvs):
        want = sc[1] if wants[i] is None else wants[i]
        attend_slab(sc[0], want, i % PARTS, kv, query, state, size, scale)
    if split:
        middle = state.shape[2] // 2
        outs[0][...] = state[:, :, :middle]
        outs[1][...] = state[:, :, middle:]


def merge_kernel(kept, came, mine, mate, own, *refs, size, rows):
    sends, mixed = refs[:-1], refs[-1]
    heads = kept.shape[0]

    @pl.when(pl.program_id(0) == 0)
    def _():
        for h in range(heads):
            other = (h + heads // 2) % heads
            first, second = kept[h, size : size + 1, :], came[other, size : size + 1, :]
            top = jnp.maximum(first, second)
            left, right = jnp.exp2(first - top), jnp.exp2(second - top)
            total = kept[h, size + 1 : size + 2, :] * left + came[other, size + 1 : size + 2, :] * right
            value = (kept[h, :size, :] * left + came[other, :size, :] * right) / total
            mixed[:, h * size : (h + 1) * size] = value.T.astype(jnp.bfloat16)

    width = mine.shape[0]
    out = jnp.dot(mixed[:, :width], mine[...], preferred_element_type=jnp.float32)
    out += jnp.dot(mixed[:, width:], mate[...], preferred_element_type=jnp.float32)
    own[...] = out[:rows, :]
    at = rows
    for send in sends:
        send[...] = out[at : at + send.shape[0], :].astype(jnp.bfloat16)
        at += send.shape[0]


def norm_kernel(own, hidden, gain, words, *refs):
    came, out = refs[:-1], refs[-1]
    stream = own[...] + hidden[...].astype(jnp.float32)
    for part in came:
        stream += part[...].astype(jnp.float32)
    width = stream.shape[1]
    square = jnp.sum(stream * stream, axis=1, keepdims=True) * (1.0 / width)
    out[:, :width] = (stream * lax.rsqrt(square + 1e-06) * gain[...]).astype(jnp.bfloat16)
    lane = lax.broadcasted_iota(jnp.int32, (stream.shape[0], out.shape[1] - width), 1)
    code = jnp.where(lane == 0, words[...] >> 8, words[...] & 255)
    out[:, width:] = code.astype(jnp.float32).astype(jnp.bfloat16)


def head_kernel(sc, *refs, block, homes, given, finish):
    parts, weight = refs[: len(homes)], refs[len(homes)]
    table, rows, codes, slots, sems = refs[-5:]
    width = weight.shape[1]
    deep = parts[0].shape[0]
    count = deep * len(homes)
    depth = slots.shape[0]
    steps = weight.shape[0] // block

    def fetch(i):
        start, slot = pl.multiple_of(i * block, 8), lax.rem(i, depth)
        source = weight.at[pl.ds(start, block), :]
        return pltpu.make_async_copy(source, slots.at[slot], sems.at[slot])

    for i in range(min(depth - 1, steps)):
        fetch(i).start()
    for i, part in enumerate(parts):
        rows[i * deep : (i + 1) * deep, :] = part[:, :width]
        codes[i * deep : (i + 1) * deep, :] = part[:, width:].astype(jnp.float32)
    turned = codes[...].T
    words = (turned[0:1, :] * 256.0 + turned[1:2, :]).astype(jnp.int32) - sc[2]
    place = lax.broadcasted_iota(jnp.int32, (block, 1), 0)

    def step(i, carry):
        top, total, weighted, picked = carry
        fetch(i).wait()

        @pl.when(i + depth - 1 < steps)
        def _():
            fetch(i + depth - 1).start()

        logits = nt(slots[lax.rem(i, depth)], rows[...])
        now = jnp.maximum(top, jnp.max(logits, axis=0, keepdims=True))
        old = jnp.exp(top - now)
        spread = jnp.exp(logits - now)
        total = total * old + jnp.sum(spread, axis=0, keepdims=True)
        weighted = weighted * old + jnp.sum(spread * logits, axis=0, keepdims=True)
        hit = place == words - i * block
        picked = picked + jnp.sum(jnp.where(hit, logits, 0.0), axis=0, keepdims=True)
        return now, total, weighted, picked

    zero = jnp.zeros((1, count), jnp.float32)
    carry = (jnp.full((1, count), NEGATIVE, jnp.float32), zero, zero, zero)
    top, total, weighted, picked = lax.fori_loop(0, steps, step, carry)
    line = lax.broadcasted_iota(jnp.int32, (STATE, count), 0)
    value = jnp.where(line == 0, top, jnp.where(line == 1, total, weighted))
    value = jnp.where(line == 3, picked, value)
    held = jnp.zeros(table.shape, jnp.float32) if not given else refs[len(homes) + 1][...]
    table[...] = held
    for i, (name, side) in enumerate(homes):
        piece = value[:, i * deep : (i + 1) * deep]
        table[sc[FACTS + name], :, side * deep : (side + 1) * deep] = piece
    if finish:
        low, high = refs[-7:-5]
        low[...] = table[: low.shape[0]]
        high[...] = table[low.shape[0] :]


def joined(mine, other):
    highest = jnp.maximum(mine[:, 0:1, :], other[:, 0:1, :])
    left, right = jnp.exp(mine[:, 0:1, :] - highest), jnp.exp(other[:, 0:1, :] - highest)
    line = lax.broadcasted_iota(jnp.int32, mine.shape, 1)
    scaled = mine * left + other * right
    return jnp.where(line == 0, highest, jnp.where(line == 3, mine + other, scaled))


def join_kernel(mine, other, low, high):
    both = joined(mine[...], other[...])
    low[...] = both[: low.shape[0]]
    high[...] = both[low.shape[0] :]


def final_kernel(sc, mine, other, logprob, entropy):
    both = joined(mine[...], other[...])[0]
    log_total = both[0:1] + jnp.log(both[1:2])
    place = lax.broadcasted_iota(jnp.int32, (1, both.shape[1]), 1) + sc[3]
    valid = place < sc[4]
    count = logprob.shape[1]
    logprob[...] = jnp.where(valid, both[3:4] - log_total, 0.0)[:, :count]
    entropy[...] = jnp.where(valid, log_total - both[2:3] / both[1:2], 0.0)[:, :count]


def smem():
    return pl.BlockSpec(memory_space=pltpu.SMEM)


def vmem():
    return pl.BlockSpec(memory_space=pltpu.VMEM)


def call(kernel, shapes, specs, limit, flops=0, read=0, **extra):
    return pl.pallas_call(
        kernel,
        out_shape=shapes,
        in_specs=specs,
        compiler_params=pltpu.CompilerParams(vmem_limit_bytes=limit * MIB),
        cost_estimate=pl.CostEstimate(flops=flops, bytes_accessed=read, transcendentals=0),
        **extra,
    )


def shape(dims, kind=jnp.float32):
    return jax.ShapeDtypeStruct(dims, kind)


def body(
    hidden,
    queries,
    rotated_rollout_keys,
    rollout_value_matrix,
    cached_key_slabs,
    cached_value_slabs,
    out_weight,
    final_gain,
    head_weight,
    token_ids,
    rollout_len,
    piece_offset,
    piece_len,
):
    groups, members = lax.axis_size("req"), lax.axis_size("mp")
    request, member = lax.axis_index("req"), lax.axis_index("mp")
    core = member % 2
    rollout, rows_here = queries.shape[0], hidden.shape[0]
    width = hidden.shape[1]
    size = rotated_rollout_keys.shape[2]
    heads_here = queries.shape[1] // size
    group_size = heads_here * members // rotated_rollout_keys.shape[1]
    value_head = member * heads_here // group_size
    scale = math.log2(math.e) / math.sqrt(size)
    heads = 2 * heads_here

    def over(block, axis, route):
        count = lax.axis_size(axis)
        pairs = [(i, route(i)) for i in range(count) if route(i) is not None]
        return lax.ppermute(block, axis, pairs)

    positions = cached_key_slabs.shape[0]
    half = positions // 2

    def half_of(slab):
        cut = slab.reshape(half // BLOCK, 2, BLOCK, slab.shape[1], size)
        cut = lax.dynamic_index_in_dim(cut, core, 1, keepdims=False)
        return lax.dynamic_index_in_dim(cut, value_head, 2, keepdims=False).reshape(half, size)

    line = lax.broadcasted_iota(jnp.int32, (META, size), 0)
    numbers = jnp.where(
        line == 0, piece_offset[0], jnp.where(line == 1, piece_len[0] // 256, piece_len[0] % 256)
    )
    all_keys, all_values = half_of(cached_key_slabs), half_of(cached_value_slabs)
    deep = half // PARTS
    kv = [
        jnp.concatenate(
            [
                all_keys[p * deep : (p + 1) * deep],
                all_values[p * deep : (p + 1) * deep],
                numbers.astype(jnp.bfloat16),
            ]
        )
        for p in range(PARTS)
    ]
    two = [over(part, "req", lambda i: (i - 2) % groups) for part in kv]
    one = [over(part, "req", lambda i: i - 1 if i % 2 else None) for part in kv]
    mate_queries = over(queries, "mp", lambda i: i ^ 1)
    mate_weight = over(out_weight, "mp", lambda i: i ^ 1)

    vocabulary_here = head_weight.shape[1]
    tour = jnp.array(ring_order(groups), jnp.int32)
    at = jnp.sum(jnp.where(tour == request, jnp.arange(groups, dtype=jnp.int32), 0))
    spots = (at + jnp.arange(groups, dtype=jnp.int32)) % groups
    match = spots[:, None] == jnp.arange(groups, dtype=jnp.int32)[None]
    homes = jnp.sum(jnp.where(match, tour[None], 0), axis=1) ^ request
    facts = [core, 3 - 2 * (request % 2), request * vocabulary_here, member * rows_here, rollout_len[0]]
    plan = jnp.concatenate([jnp.stack(facts).astype(jnp.int32), homes])

    order = list(range(0, members, 2)) + list(range(1, members, 2))

    def arrange(block):
        return [lax.dynamic_slice_in_dim(block, (member ^ k) * rows_here, rows_here) for k in order]

    query = jnp.concatenate(
        [jnp.concatenate(arrange(part)) for part in (queries, mate_queries)], axis=1
    )
    times = jnp.concatenate(
        [(member ^ k) * rows_here + jnp.arange(rows_here, dtype=jnp.int32) for k in order]
    )[None]

    def own_half(block):
        cut = lax.dynamic_index_in_dim(block, value_head, 1, keepdims=False)
        return lax.dynamic_slice_in_dim(cut, core * (rollout // 2), rollout // 2)

    full = shape((heads, size + STATE, rollout))
    part = shape((heads, size + STATE, rollout // 2))
    work = 4 * heads * rollout * half * size
    state = call(
        functools.partial(first_kernel, size=size, scale=scale),
        full,
        [smem()] + [vmem()] * (4 + PARTS),
        32,
        work,
        2 * half * size * 4,
    )(
        plan,
        times,
        query,
        own_half(rotated_rollout_keys),
        own_half(rollout_value_matrix),
        *kv,
    )
    first_two, state = lax.optimization_barrier((two[0], state))
    second_two, one = lax.optimization_barrier((two[1:], one))
    swap = [over(part, "req", lambda i: i ^ 1) for part in (first_two, *second_two)]
    three = [over(part, "req", lambda i: (i - 2) % groups if i % 2 else None) for part in swap]
    state = call(
        functools.partial(more_kernel, size=size, scale=scale, wants=(1,) * PARTS + (2,) * PARTS, split=False),
        full,
        [smem()] + [vmem()] * (2 + 2 * PARTS),
        32,
        2 * work,
        4 * half * size * 4,
    )(plan, query, *one, *two, state)
    state = call(
        functools.partial(more_kernel, size=size, scale=scale, wants=(None,) * PARTS, split=False),
        full,
        [smem()] + [vmem()] * (2 + PARTS),
        32,
        work,
        2 * half * size * 4,
    )(plan, query, *swap, state)
    kept, sent = call(
        functools.partial(more_kernel, size=size, scale=scale, wants=(3,) * PARTS, split=True),
        (part, part),
        [smem()] + [vmem()] * (2 + PARTS),
        32,
        work,
        2 * half * size * 4,
        scratch_shapes=[pltpu.VMEM(full.shape, jnp.float32)],
    )(plan, query, *three, state)
    came = over(sent, "mp", lambda i: i ^ 1)

    tile = 2048
    rows_core = rollout // 2
    deep = rows_here // 2
    pieces = [(k, side) for k in range(1, members // 2) for side in (0, 1)]
    own, *sends = pl.pallas_call(
        functools.partial(merge_kernel, size=size, rows=rows_here),
        out_shape=(shape((rows_here, width)), *[shape((deep, width), jnp.bfloat16)] * len(pieces)),
        grid=(width // tile,),
        in_specs=[
            pl.BlockSpec(part.shape, lambda i: (0, 0, 0)),
            pl.BlockSpec(part.shape, lambda i: (0, 0, 0)),
            pl.BlockSpec((out_weight.shape[0], tile), lambda i: (0, i)),
            pl.BlockSpec((out_weight.shape[0], tile), lambda i: (0, i)),
        ],
        out_specs=(
            pl.BlockSpec((rows_here, tile), lambda i: (0, i)),
            *[pl.BlockSpec((deep, tile), lambda i: (0, i))] * len(pieces),
        ),
        scratch_shapes=[pltpu.VMEM((rows_core, heads * size), jnp.bfloat16)],
        compiler_params=pltpu.CompilerParams(vmem_limit_bytes=24 * MIB),
        cost_estimate=pl.CostEstimate(
            flops=2 * rows_core * heads * size * width,
            bytes_accessed=4 * out_weight.shape[0] * width,
            transcendentals=0,
        ),
    )(kept, came, out_weight, mate_weight)

    ring = ring_order(groups)
    place = {group: at for at, group in enumerate(ring)}

    def ahead(block):
        return over(block, "req", lambda i: ring[(place[i] + 1) % groups])

    def behind(block):
        return over(block, "req", lambda i: ring[(place[i] - 1) % groups])

    def normed(side):
        came = [
            over(block, "mp", lambda i, k=k: i ^ (2 * k))
            for (k, half_side), block in zip(pieces, sends)
            if half_side == side
        ]

        def cut(columns):
            return pl.BlockSpec((deep, columns), lambda i: (side, 0))

        return pl.pallas_call(
            norm_kernel,
            out_shape=shape((deep, width + size), jnp.bfloat16),
            grid=(1,),
            in_specs=[cut(width), cut(width), pl.BlockSpec((1, width), lambda i: (0, 0)), cut(1)]
            + [pl.BlockSpec((deep, width), lambda i: (0, 0))] * len(came),
            out_specs=pl.BlockSpec((deep, width + size), lambda i: (0, 0)),
            compiler_params=pltpu.CompilerParams(vmem_limit_bytes=8 * MIB),
            cost_estimate=pl.CostEstimate(
                flops=0, bytes_accessed=deep * width * 8, transcendentals=0
            ),
        )(own, hidden, final_gain[None], token_ids[:, None], *came)

    weight = head_weight.T
    block = 400 if vocabulary_here % 400 == 0 else vocabulary_here
    forth, back = [None, None], [None, None]
    ready = [[], []]
    for side in (0, 1):
        forth[side] = back[side] = normed(side)
        ready[side].append((0, side, forth[side]))
    for step in range(1, groups // 2):
        for side in (0, 1):
            forth[side], back[side] = ahead(forth[side]), behind(back[side])
            ready[side] += [(-step % groups, side, forth[side]), (step, side, back[side])]
    final = [(groups // 2, 0, ahead(forth[0])), (groups // 2, 1, behind(back[1]))]
    own_rows, *_ = lax.optimization_barrier((ready[0][0][2], forth[1], back[1]))
    ready[0][0] = (0, 0, own_rows)
    arrived = ready[0] + ready[1] + final
    batch = max(1, 256 // deep)
    depth = 4
    table = None
    whole, halves = shape((groups, STATE, 128)), shape((groups // 2, STATE, 128))
    for at in range(0, len(arrived), batch):
        now = arrived[at : at + batch]
        count = deep * len(now)
        given = [] if table is None else [table]
        done = at + batch >= len(arrived)
        table = call(
            functools.partial(
                head_kernel,
                block=block,
                homes=[(name, side) for name, side, _ in now],
                given=len(given),
                finish=done,
            ),
            (halves, halves) if done else whole,
            [smem()]
            + [vmem()] * len(now)
            + [pl.BlockSpec(memory_space=pl.ANY)]
            + [vmem()] * len(given),
            44,
            2 * count * width * vocabulary_here,
            2 * width * vocabulary_here,
            scratch_shapes=[pltpu.VMEM(whole.shape, jnp.float32)] * done
            + [
                pltpu.VMEM((count, width), jnp.bfloat16),
                pltpu.VMEM((count, size), jnp.float32),
                pltpu.VMEM((depth, block, width), jnp.bfloat16),
                pltpu.SemaphoreType.DMA((depth,)),
            ],
        )(plan, *[rows for _, _, rows in now], weight, *given)
    mine, away = table
    bit = groups // 2
    while bit > 1:
        other = over(away, "req", lambda i, bit=bit: i ^ bit)
        bit //= 2
        part = shape((bit, STATE, 128))
        mine, away = call(join_kernel, (part, part), [vmem()] * 2, 4)(mine, other)
    other = over(away, "req", lambda i: i ^ 1)
    rows_out = shape((1, rows_here))
    logprob, entropy = call(final_kernel, (rows_out, rows_out), [smem()] + [vmem()] * 2, 4)(
        plan, mine, other
    )
    return (logprob.reshape(rows_here), entropy.reshape(rows_here))


def solution(mesh):
    placed = (
        P(("req", "mp"), None),
        P("req", "mp"),
        P("req", None, None),
        P("req", None, None),
        P("req", None, None),
        P("req", None, None),
        P("mp", None),
        P(),
        P(None, "req"),
        P(("req", "mp")),
        P("req"),
        P("req"),
        P("req"),
    )
    return jax.shard_map(
        body,
        mesh=mesh,
        in_specs=placed,
        out_specs=(P(("req", "mp")), P(("req", "mp"))),
        check_vma=False,
    )
```
